1024 devices in a mesh: row: 32 (over x, z_hi, core), col: 32 (over z_lo, y).
Axes of the slice: x: 4, y: 4, z: 32 (z_hi: 4, z_lo: 8; z = z_hi * 8 + z_lo), core: 2. Of those that a mesh axis runs over, the one named last changes fastest.
Arguments:
- stem: bfloat16 [2, 512, 131072], P(None, None, ('row', 'col')), may hold values from -6 to 6
- left_pool: bfloat16 [32, 2, 512, 512], P('row'), may hold values from -0.1875 to 0.1875
- right_pool: bfloat16 [32, 2, 2, 512, 512], P('row'), may hold values from -0.1875 to 0.1875
- owners: int32 [3], replicated, may hold values from 0 to 31, as said below
- slices: int32 [3], replicated, may hold values from 0 to 1, as said below
- relabels: int32 [2, 512], replicated, may hold values from 0 to 511, each once within a row
Outputs:
- amplitudes: bfloat16 [2, 512, 131072], P(None, None, ('row', 'col'))
The draws below stay inside these ranges and needn't reach their ends.
Inputs may be any that keep to these rules, and one draw needn't show every extreme that they name: `owners`: the 3 entries are distinct pool entries. `slices`: the 3 entries are not all equal.
All inputs are finite; a program needn't handle non-finite values.
Results may differ from the reference program's by a relative error of at most 0.0075.
Values may be sent and summed in bfloat16 or wider, within the bound.
No kernel may reach another device: no remote copies, remote signals or barrier semaphores. Data moves between devices by JAX's collectives and lax.ppermute only.
A program may use at most 32 MiB of HBM per device.

```python
import jax
import jax.numpy as jnp

W = 512
SR = 128
CONTRACTIONS = 3
SLICES = 2
POOL = 32
ROWS = 131072
N_ROW = 32
N_COL = 32


def draw_owners(key, part):
    return jax.random.permutation(key, POOL)[:CONTRACTIONS].astype(jnp.int32)


def draw_slices(key, part):
    values = jax.random.randint(jax.random.fold_in(key, 11), (CONTRACTIONS,), 0, SLICES).astype(jnp.int32)
    where = jax.random.randint(jax.random.fold_in(key, 12), (), 1, CONTRACTIONS).astype(jnp.int32)
    other = ((values[0] + 1) % SLICES).astype(jnp.int32)
    return values.at[where].set(other).astype(jnp.int32)


def steps_of(own_key, shape, pieces, low, largest):
    factor_of, own = 1.0, jax.random.fold_in(own_key, 6)
    for dim, shards_of in pieces:
        draws = jnp.exp(jax.random.uniform(jax.random.fold_in(own, dim), (shards_of,), jnp.float32, low / len(pieces), largest / len(pieces)))
        factor_of = factor_of * jnp.repeat(draws, shape[dim] // shards_of).reshape([-1 if axis == dim else 1 for axis in range(len(shape))])
    return factor_of


def scatter_about(stream_key, extent, scale, most, shards=(), held_as=jnp.bfloat16):
    array = jax.random.normal(stream_key, extent, jnp.float32) * scale
    if len(shards) > 0:
        array = steps_of(stream_key, extent, shards, -0.22, 0.18) * array
    return jnp.clip(array, min=-most, max=most).astype(held_as)


def setup_inputs(seed: int = 0) -> dict:
    keys = jax.random.split(jax.random.key(seed), 7)
    stem = scatter_about(keys[0], (2, W, ROWS), 1.0, 6.0, ((2, 1024),))
    left_pool = scatter_about(keys[1], (POOL, 2, W, W), (2 * W) ** -0.5, 0.1875, ((0, 32),))
    right_pool = scatter_about(keys[2], (POOL, SLICES, 2, W, W), (2 * W) ** -0.5, 0.1875, ((0, 32),))
    owners = draw_owners(jax.random.fold_in(keys[6], 71), 0)
    slices = draw_slices(jax.random.fold_in(keys[6], 71), 0)
    relabels = jax.vmap(lambda own: jax.random.permutation(own, W))(jax.random.split(keys[5], (CONTRACTIONS - 1))).reshape((CONTRACTIONS - 1, W)).astype(jnp.int32)
    return dict(stem=stem, left_pool=left_pool, right_pool=right_pool, owners=owners, slices=slices, relabels=relabels)


def complex_product(first, second):
    real = jnp.dot(first[0], second[0], preferred_element_type=jnp.float32) - jnp.dot(first[1], second[1], preferred_element_type=jnp.float32)
    imaginary = jnp.dot(first[0], second[1], preferred_element_type=jnp.float32) + jnp.dot(first[1], second[0], preferred_element_type=jnp.float32)
    return jnp.stack([real, imaginary]).astype(jnp.bfloat16)


def regroup(state):
    total = state.shape[2]
    blocks = state.reshape(2, N_COL, W // N_COL, N_ROW, N_COL, SR)
    return jnp.swapaxes(blocks, 1, 4).reshape(2, W, total)


def reference(stem, left_pool, right_pool, owners, slices, relabels):
    branches = []
    for section in range(CONTRACTIONS):
        branches.append(complex_product(left_pool[owners[section]], right_pool[owners[section], slices[section]]))
    state = complex_product(branches[0], stem)
    for section in range(1, CONTRACTIONS):
        state = jnp.take(regroup(state), relabels[section - 1], axis=1)
        state = complex_product(branches[section], state)
    return state
```

```python
import functools

import jax
import jax.numpy as jnp
from jax import lax
from jax.experimental import pallas as pl
from jax.experimental.pallas import tpu as pltpu
from jax.sharding import Mesh
from jax.sharding import PartitionSpec as P

PARTS = (("x", 4), ("zh", 4), ("core", 2), ("zl", 8), ("y", 4))
ALL = tuple(name for name, _ in PARTS)
ROW, COL = ALL[:3], ALL[3:]
SPREAD, PLANE = ("x", "core"), ("x", "y")
TILE = (16, 128)
F32, BF16 = jnp.float32, jnp.bfloat16


def own_row():
    return (lax.axis_index("x") * 4 + lax.axis_index("zh")) * 2 + lax.axis_index("core")


def slice_kernel(owners, slices, relabels, left, right, out):
    row = own_row()
    used = [owners[k] == row for k in range(3)]
    chosen = jnp.int32(0)
    for k in range(3):
        chosen = jnp.where(used[k], slices[k], chosen)
    block = lax.axis_index("y") * 8 + lax.axis_index("zl")
    rows = pl.ds(pl.multiple_of(block * 16, 16), 16)
    both = jnp.concatenate([left[0, 0, rows, :], left[0, 1, rows, :]], axis=0)
    by_real = jnp.dot(both, right[0, chosen, 0], preferred_element_type=F32)
    by_imag = jnp.dot(both, right[0, chosen, 1], preferred_element_type=F32)
    real = by_real[:16] - by_imag[16:]
    imag = by_imag[:16] + by_real[16:]
    branch = jnp.concatenate([real, imag], axis=0).astype(BF16)
    place = lax.broadcasted_iota(jnp.int32, (512, 512), 0)
    mapping = lax.broadcasted_iota(jnp.int32, (1, 512), 1)
    mapping = jnp.where(used[1], relabels[0:1, :], mapping)
    mapping = jnp.where(used[2], relabels[1:2, :], mapping)
    onehot = jnp.where(place == mapping, 1.0, 0.0).astype(BF16)
    moved = lax.dot_general(branch, onehot, (((1,), (1,)), ((), ())), preferred_element_type=F32).astype(BF16)
    for part in range(2):
        for block in range(4):
            out[block * 2 + part] = moved[part * 16 : part * 16 + 16, block * 128 : block * 128 + 128]


def branch_slice(owners, slices, relabels, left, right):
    smem, vmem = pl.BlockSpec(memory_space=pltpu.SMEM), pl.BlockSpec(memory_space=pltpu.VMEM)
    return pl.pallas_call(
        slice_kernel,
        in_specs=[smem, smem, vmem, vmem, vmem],
        out_specs=vmem,
        out_shape=jax.ShapeDtypeStruct((8, *TILE), BF16),
        name="branch_slice",
    )(owners, slices, relabels, left, right)


def contract_kernel(own, other, state, out, *, pick):
    parts = []
    for ref in (own, other):
        value = ref[...] if pick is None else ref[:, :, pick]
        columns = [value[c * 4 : c * 4 + 4].reshape(512, 128) for c in range(4)]
        parts.append(jnp.concatenate(columns, axis=1))
    if len(state.shape) == 4:
        real, imag = state[:, 0].reshape(512, 128), state[:, 1].reshape(512, 128)
    else:
        real, imag = state[0], state[1]
    both = jnp.concatenate([real, imag], axis=1)
    by_own = jnp.dot(parts[0], both, preferred_element_type=F32)
    by_other = jnp.dot(parts[1], both, preferred_element_type=F32)
    swapped = lax.axis_index("core") == 1
    by_real = jnp.where(swapped, by_other, by_own)
    by_imag = jnp.where(swapped, by_own, by_other)
    real = (by_real[:, :128] - by_imag[:, 128:]).astype(BF16)
    imag = (by_real[:, 128:] + by_imag[:, :128]).astype(BF16)
    if len(out.shape) == 4:
        out[:, 0] = real.reshape(32, *TILE)
        out[:, 1] = imag.reshape(32, *TILE)
    else:
        out[0] = real
        out[1] = imag


def contract(own, other, state, shape, pick=None):
    vmem = pl.BlockSpec(memory_space=pltpu.VMEM)
    return pl.pallas_call(
        functools.partial(contract_kernel, pick=pick),
        in_specs=[vmem, vmem, vmem],
        out_specs=vmem,
        out_shape=jax.ShapeDtypeStruct(shape, BF16),
        compiler_params=pltpu.CompilerParams(vmem_limit_bytes=16 << 20),
        name="contract",
    )(own, other, state)


def send(blocks, axes):
    return lax.all_to_all(blocks, axes, 0, 0, tiled=True)


def to_all(block, axes, count):
    return send(jnp.broadcast_to(block[None], (count, *block.shape)), axes)


def body(stem, left, right, owners, slices, relabels):
    at_x, at_zh, at_core = owners // 8, (owners // 2) % 4, owners % 2
    tiles = send(branch_slice(owners, slices, relabels, left, right), SPREAD)
    mine = [lax.dynamic_index_in_dim(tiles, at_x[k] * 2 + at_core[k], 0, keepdims=False) for k in range(3)]
    shares = to_all(jnp.stack(mine), "zh", 4)
    shares = jnp.stack([lax.dynamic_index_in_dim(shares, at_zh[k], 0, keepdims=False)[k] for k in range(3)])
    shares = to_all(shares, "zl", 8)
    held = to_all(shares, PLANE, 16)
    first, rest = held[:, :, 0], held[:, :, 1:]
    first_other, rest_other = (lax.ppermute(part, "core", [(0, 1), (1, 0)]) for part in (first, rest))
    state = contract(first, first_other, stem, (32, 2, *TILE))
    state = contract(rest, rest_other, send(state, COL), (32, 2, *TILE), 0)
    return contract(rest, rest_other, send(state, COL), (2, 512, 128), 1)


def solution(mesh):
    fine = Mesh(mesh.devices.reshape([size for _, size in PARTS]), ALL)
    in_specs = (
        P(None, None, ALL),
        P(ROW, None, None, None),
        P(ROW, None, None, None, None),
        P(),
        P(),
        P(),
    )
    return jax.shard_map(body, mesh=fine, in_specs=in_specs, out_specs=P(None, None, ALL), check_vma=False)
```

```python
import jax
import jax.numpy as jnp
from jax import lax
from jax.experimental import pallas as pl
from jax.experimental.pallas import tpu as pltpu
from jax.sharding import Mesh
from jax.sharding import PartitionSpec as P

PARTS = (("x", 4), ("zh", 4), ("core", 2), ("za", 2), ("zb", 4), ("y", 4))
ALL = tuple(name for name, _ in PARTS)
ROW, COL = ALL[:3], ALL[3:]
SPREAD, LINE, PLANE, NEAR = ("x", "core"), ("za", "zb"), ("x", "y"), ("core", "zb", "y")
TILE = (16, 128)
FLIP = [(0, 1), (1, 0)]
F32, BF16 = jnp.float32, jnp.bfloat16


def own_row():
    return (lax.axis_index("x") * 4 + lax.axis_index("zh")) * 2 + lax.axis_index("core")


def slice_kernel(owners, slices, relabels, left, right, out):
    row = own_row()
    used = [owners[k] == row for k in range(3)]
    chosen = jnp.int32(0)
    for k in range(3):
        chosen = jnp.where(used[k], slices[k], chosen)
    at_z, at_y = lax.axis_index("za") * 4 + lax.axis_index("zb"), lax.axis_index("y")
    block = jnp.where(used[0], at_z * 4 + at_y, at_y * 8 + at_z)
    rows = pl.ds(pl.multiple_of(block * 16, 16), 16)
    both = jnp.concatenate([left[0, 0, rows, :], left[0, 1, rows, :]], axis=0)
    by_real = jnp.dot(both, right[0, chosen, 0], preferred_element_type=F32)
    by_imag = jnp.dot(both, right[0, chosen, 1], preferred_element_type=F32)
    real = by_real[:16] - by_imag[16:]
    imag = by_imag[:16] + by_real[16:]
    branch = jnp.concatenate([real, imag], axis=0).astype(BF16)
    q = lax.broadcasted_iota(jnp.int32, (512, 512), 0)
    arrived = (((q >> 3) & 1) << 8) | (((q >> 4) & 15) << 4) | (((q >> 8) & 1) << 3) | (q & 7)
    place = jnp.where(used[1], arrived, q)
    mapping = lax.broadcasted_iota(jnp.int32, (1, 512), 1)
    mapping = jnp.where(used[1], relabels[0:1, :], mapping)
    mapping = jnp.where(used[2], relabels[1:2, :], mapping)
    onehot = jnp.where(place == mapping, 1.0, 0.0).astype(BF16)
    moved = lax.dot_general(branch, onehot, (((1,), (1,)), ((), ())), preferred_element_type=F32)
    halves = jnp.concatenate([moved[:8], moved[16:24], moved[8:16], moved[24:]], axis=0)
    moved = jnp.where(used[0], halves, moved).astype(BF16)
    for c in range(4):
        for h in range(2):
            out[c * 2 + h] = moved[h * 16 : h * 16 + 16, c * 128 : c * 128 + 128]


VMEM = pl.BlockSpec(memory_space=pltpu.VMEM)
SMEM = pl.BlockSpec(memory_space=pltpu.SMEM)
SMALL = pltpu.CompilerParams(vmem_limit_bytes=16 << 20)


def branch_slice(owners, slices, relabels, left, right):
    return pl.pallas_call(
        slice_kernel,
        in_specs=[SMEM, SMEM, VMEM, VMEM, VMEM],
        out_specs=VMEM,
        out_shape=jax.ShapeDtypeStruct((8, *TILE), BF16),
        name="branch_slice",
    )(owners, slices, relabels, left, right)


def first_kernel(held, *refs):
    *stems, out = refs
    branch = jnp.concatenate([held[c * 4 : c * 4 + 4, :4].reshape(256, 128) for c in range(4)], axis=1)
    results = []
    for stem in stems:
        both = jnp.concatenate([stem[0], stem[1]], axis=1)
        by = jnp.dot(branch, both, preferred_element_type=F32).reshape(16, 2, 8, 256)
        real = by[:, 0, :, :128] - by[:, 1, :, 128:]
        imag = by[:, 0, :, 128:] + by[:, 1, :, :128]
        results.append((real, imag))
    core, ahead = lax.axis_index("core"), lax.axis_index("za") == 1
    for flip in range(2):
        target = jnp.bitwise_xor(core, flip)
        for part in range(2):
            near, far = results[flip][part], results[2 + flip][part]
            low, high = jnp.where(ahead, far, near), jnp.where(ahead, near, far)
            tiles = jnp.concatenate([low, high], axis=1).astype(BF16)
            for y in range(4):
                for zb in range(4):
                    out[target, zb * 4 + y, part] = tiles[y * 4 + zb]


def first_contract(held, stems):
    return pl.pallas_call(
        first_kernel,
        in_specs=[VMEM] * 5,
        out_specs=VMEM,
        out_shape=jax.ShapeDtypeStruct((2, 16, 2, *TILE), BF16),
        compiler_params=SMALL,
        name="first_contract",
    )(held, *stems)


def make_contract_kernel(pick):
    def kernel(own, other, state, out):
        parts = []
        for ref in (own, other):
            columns = [ref[c * 4 : c * 4 + 4, pick].reshape(512, 128) for c in range(4)]
            parts.append(jnp.concatenate(columns, axis=1))
        both = jnp.concatenate([state[:, 0].reshape(512, 128), state[:, 1].reshape(512, 128)], axis=1)
        by_own = jnp.dot(parts[0], both, preferred_element_type=F32)
        by_other = jnp.dot(parts[1], both, preferred_element_type=F32)
        swapped = lax.axis_index("core") == 1
        by_real = jnp.where(swapped, by_other, by_own)
        by_imag = jnp.where(swapped, by_own, by_other)
        real = (by_real[:, :128] - by_imag[:, 128:]).astype(BF16)
        imag = (by_real[:, 128:] + by_imag[:, :128]).astype(BF16)
        if len(out.shape) == 4:
            out[:, 0] = real.reshape(32, *TILE)
            out[:, 1] = imag.reshape(32, *TILE)
        else:
            out[0] = real
            out[1] = imag

    return kernel


def contract(own, other, state, shape, pick):
    return pl.pallas_call(
        make_contract_kernel(pick),
        in_specs=[VMEM] * 3,
        out_specs=VMEM,
        out_shape=jax.ShapeDtypeStruct(shape, BF16),
        compiler_params=SMALL,
        name="contract",
    )(own, other, state)


def send(blocks, axes):
    return lax.all_to_all(blocks, axes, 0, 0, tiled=True)


def to_all(block, axes, count):
    return send(jnp.broadcast_to(block[None], (count, *block.shape)), axes)


def body(stem, left, right, owners, slices, relabels):
    at_x, at_zh, at_core = owners // 8, (owners // 2) % 4, owners % 2
    across = lax.ppermute(stem, "za", FLIP)
    stems = (stem, lax.ppermute(stem, "core", FLIP), across, lax.ppermute(across, "core", FLIP))
    tiles = send(branch_slice(owners, slices, relabels, left, right), SPREAD)
    mine = [lax.dynamic_index_in_dim(tiles, at_x[k] * 2 + at_core[k], 0, keepdims=False) for k in range(3)]
    shares = to_all(jnp.stack(mine), "zh", 4)
    shares = jnp.stack([lax.dynamic_index_in_dim(shares, at_zh[k], 0, keepdims=False)[k] for k in range(3)])
    shares = to_all(shares, LINE, 8)
    first = lax.dynamic_slice_in_dim(shares[:, 0], lax.axis_index("za") * 4, 4, 0)
    held = to_all(jnp.concatenate([first, shares[:, 1], shares[:, 2]]), PLANE, 16)
    state = first_contract(held, stems).reshape(32, 2, *TILE)
    own = held[:, 4:].reshape(16, 2, 8, *TILE)
    other = lax.ppermute(own, "core", FLIP)
    state = contract(own, other, send(state, NEAR), (32, 2, *TILE), 0)
    return contract(own, other, send(state, COL), (2, 512, 128), 1)


def solution(mesh):
    fine = Mesh(mesh.devices.reshape([size for _, size in PARTS]), ALL)
    in_specs = (
        P(None, None, ALL),
        P(ROW, None, None, None),
        P(ROW, None, None, None, None),
        P(),
        P(),
        P(),
    )
    return jax.shard_map(body, mesh=fine, in_specs=in_specs, out_specs=P(None, None, ALL), check_vma=False)
```

```python
import functools

import jax
import jax.numpy as jnp
from jax import lax
from jax.experimental import pallas as pl
from jax.experimental.pallas import tpu as pltpu
from jax.sharding import Mesh
from jax.sharding import PartitionSpec as P

PARTS = (("x", 4), ("zh", 4), ("core", 2), ("za", 2), ("zb", 4), ("y", 4))
ALL = tuple(name for name, _ in PARTS)
ROW, COL = ALL[:3], ALL[3:]
SPREAD, LINE, PLANE, NEAR = ("x", "core"), ("za", "zb"), ("x", "y"), ("core", "zb", "y")
TILE = (16, 128)
FLIP = [(0, 1), (1, 0)]
F32, BF16 = jnp.float32, jnp.bfloat16


def own_row():
    return (lax.axis_index("x") * 4 + lax.axis_index("zh")) * 2 + lax.axis_index("core")


def slice_kernel(owners, slices, relabels, left, right, out, l_own, r_own, sems):
    row = own_row()
    used = [owners[k] == row for k in range(3)]
    chosen = jnp.int32(0)
    for k in range(3):
        chosen = jnp.where(used[k], slices[k], chosen)
    at_z, at_y = lax.axis_index("za") * 4 + lax.axis_index("zb"), lax.axis_index("y")
    block = jnp.where(used[0], at_z * 4 + at_y, at_y * 8 + at_z)
    rows = pl.ds(pl.multiple_of(block * 16, 16), 16)
    copies = [
        pltpu.make_async_copy(right.at[0, chosen, 0], r_own.at[0], sems.at[0]),
        pltpu.make_async_copy(right.at[0, chosen, 1], r_own.at[1], sems.at[1]),
        pltpu.make_async_copy(left.at[0, 0, rows], l_own.at[0], sems.at[2]),
        pltpu.make_async_copy(left.at[0, 1, rows], l_own.at[1], sems.at[3]),
    ]
    for copy in copies:
        copy.start()
    q = lax.broadcasted_iota(jnp.int32, (512, 512), 0)
    arrived = (((q >> 3) & 1) << 8) | (((q >> 4) & 15) << 4) | (((q >> 8) & 1) << 3) | (q & 7)
    place = jnp.where(used[1], arrived, q)
    mapping = lax.broadcasted_iota(jnp.int32, (1, 512), 1)
    mapping = jnp.where(used[1], relabels[0:1, :], mapping)
    mapping = jnp.where(used[2], relabels[1:2, :], mapping)
    onehot = jnp.where(place == mapping, 1.0, 0.0).astype(BF16)
    for copy in copies:
        copy.wait()
    both = jnp.concatenate([l_own[0], l_own[1]], axis=0)
    by_real = jnp.dot(both, r_own[0], preferred_element_type=F32)
    by_imag = jnp.dot(both, r_own[1], preferred_element_type=F32)
    real = by_real[:16] - by_imag[16:]
    imag = by_imag[:16] + by_real[16:]
    branch = jnp.concatenate([real, imag], axis=0).astype(BF16)
    moved = lax.dot_general(branch, onehot, (((1,), (1,)), ((), ())), preferred_element_type=F32)
    halves = jnp.concatenate([moved[:8], moved[16:24], moved[8:16], moved[24:]], axis=0)
    moved = jnp.where(used[0], halves, moved).astype(BF16)
    for c in range(4):
        for h in range(2):
            out[c * 2 + h] = moved[h * 16 : h * 16 + 16, c * 128 : c * 128 + 128]


VMEM = pl.BlockSpec(memory_space=pltpu.VMEM)
HBM = pl.BlockSpec(memory_space=pl.ANY)
SMEM = pl.BlockSpec(memory_space=pltpu.SMEM)
SMALL = pltpu.CompilerParams(vmem_limit_bytes=16 << 20)


def branch_slice(owners, slices, relabels, left, right):
    return pl.pallas_call(
        slice_kernel,
        in_specs=[SMEM, SMEM, VMEM, HBM, HBM],
        out_specs=VMEM,
        scratch_shapes=[
            pltpu.VMEM((2, 16, 512), BF16),
            pltpu.VMEM((2, 512, 512), BF16),
            pltpu.SemaphoreType.DMA((4,)),
        ],
        out_shape=jax.ShapeDtypeStruct((8, *TILE), BF16),
        name="branch_slice",
    )(owners, slices, relabels, left, right)


def pick_kernel(by_zh, owners, tiles, out):
    for k in range(3):
        at_x, at_zh, at_core = owners[k] >> 3, (owners[k] >> 1) & 3, owners[k] & 1
        tile = tiles[at_zh, k] if by_zh else tiles[at_x * 2 + at_core]
        for i in range(out.shape[0]):
            out[i, k] = tile


def pick(owners, tiles, by_zh, count):
    return pl.pallas_call(
        functools.partial(pick_kernel, by_zh),
        in_specs=[SMEM, VMEM],
        out_specs=VMEM,
        out_shape=jax.ShapeDtypeStruct((count, 3, *TILE), BF16),
        compiler_params=SMALL,
        name="pick",
    )(owners, tiles)


def pack_kernel(tiles, out):
    half = lax.axis_index("za") * 4
    for j in range(20):
        tile = tiles[half + j, 0] if j < 4 else tiles[(j - 4) % 8, 1 + (j - 4) // 8]
        for i in range(16):
            out[i, j] = tile


def pack(tiles):
    return pl.pallas_call(
        pack_kernel,
        in_specs=[VMEM],
        out_specs=VMEM,
        out_shape=jax.ShapeDtypeStruct((16, 20, *TILE), BF16),
        compiler_params=SMALL,
        name="pack",
    )(tiles)


def first_kernel(held, *refs):
    *stems, out = refs
    branch = jnp.concatenate([held[c * 4 : c * 4 + 4, :4].reshape(256, 128) for c in range(4)], axis=1)
    results = []
    for stem in stems:
        both = jnp.concatenate([stem[0], stem[1]], axis=1)
        by = jnp.dot(branch, both, preferred_element_type=F32).reshape(16, 2, 8, 256)
        real = by[:, 0, :, :128] - by[:, 1, :, 128:]
        imag = by[:, 0, :, 128:] + by[:, 1, :, :128]
        results.append((real, imag))
    core, ahead = lax.axis_index("core"), lax.axis_index("za") == 1
    for flip in range(2):
        target = jnp.bitwise_xor(core, flip)
        for part in range(2):
            near, far = results[flip][part], results[2 + flip][part]
            low, high = jnp.where(ahead, far, near), jnp.where(ahead, near, far)
            tiles = jnp.concatenate([low, high], axis=1).astype(BF16)
            for y in range(4):
                for zb in range(4):
                    out[target, zb * 4 + y, part] = tiles[y * 4 + zb]


def first_contract(held, stems):
    return pl.pallas_call(
        first_kernel,
        in_specs=[VMEM] * 5,
        out_specs=VMEM,
        out_shape=jax.ShapeDtypeStruct((2, 16, 2, *TILE), BF16),
        compiler_params=SMALL,
        name="first_contract",
    )(held, *stems)


def make_contract_kernel(pick):
    def kernel(own, other, state, out):
        parts = []
        for ref in (own, other):
            columns = [ref[c * 4 : c * 4 + 4, pick].reshape(512, 128) for c in range(4)]
            parts.append(jnp.concatenate(columns, axis=1))
        both = jnp.concatenate([state[:, 0].reshape(512, 128), state[:, 1].reshape(512, 128)], axis=1)
        by_own = jnp.dot(parts[0], both, preferred_element_type=F32)
        by_other = jnp.dot(parts[1], both, preferred_element_type=F32)
        swapped = lax.axis_index("core") == 1
        by_real = jnp.where(swapped, by_other, by_own)
        by_imag = jnp.where(swapped, by_own, by_other)
        real = (by_real[:, :128] - by_imag[:, 128:]).astype(BF16)
        imag = (by_real[:, 128:] + by_imag[:, :128]).astype(BF16)
        if len(out.shape) == 4:
            out[:, 0] = real.reshape(32, *TILE)
            out[:, 1] = imag.reshape(32, *TILE)
        else:
            out[0] = real
            out[1] = imag

    return kernel


def contract(own, other, state, shape, pick):
    return pl.pallas_call(
        make_contract_kernel(pick),
        in_specs=[VMEM] * 3,
        out_specs=VMEM,
        out_shape=jax.ShapeDtypeStruct(shape, BF16),
        compiler_params=SMALL,
        name="contract",
    )(own, other, state)


def send(blocks, axes):
    return lax.all_to_all(blocks, axes, 0, 0, tiled=True)


def steps(stem, left, right, owners, slices, relabels):
    across = lax.ppermute(stem, "za", FLIP)
    beside = lax.ppermute(stem, "core", FLIP)
    both = lax.ppermute(across, "core", FLIP)
    made = branch_slice(owners, slices, relabels, left, right)
    tiles = send(made, SPREAD)
    picked = pick(owners, tiles, False, 4)
    shares = send(picked, "zh")
    picked = pick(owners, shares, True, 8)
    shares = send(picked, LINE)
    packed = pack(shares)
    held = send(packed, PLANE)
    state = first_contract(held, (stem, beside, across, both)).reshape(32, 2, *TILE)
    own = held[:, 4:].reshape(16, 2, 8, *TILE)
    other = lax.ppermute(own, "core", FLIP)
    state = contract(own, other, send(state, NEAR), (32, 2, *TILE), 0)
    return contract(own, other, send(state, COL), (2, 512, 128), 1)


def solution(mesh):
    fine = Mesh(mesh.devices.reshape([size for _, size in PARTS]), ALL)
    in_specs = (
        P(None, None, ALL),
        P(ROW, None, None, None),
        P(ROW, None, None, None, None),
        P(),
        P(),
        P(),
    )
    return jax.shard_map(steps, mesh=fine, in_specs=in_specs, out_specs=P(None, None, ALL), check_vma=False)
```

```python
import functools

import jax
import jax.numpy as jnp
from jax import lax
from jax.experimental import pallas as pl
from jax.experimental.pallas import tpu as pltpu
from jax.sharding import Mesh
from jax.sharding import PartitionSpec as P

PARTS = (("x", 4), ("zh", 4), ("core", 2), ("za", 2), ("zb", 4), ("y", 4))
ALL = tuple(name for name, _ in PARTS)
ROW, COL = ALL[:3], ALL[3:]
SPREAD, LINE, PLANE, NEAR = ("x", "core"), ("za", "zb"), ("x", "y"), ("core", "zb", "y")
TILE = (16, 128)
FLIP = [(0, 1), (1, 0)]
F32, BF16 = jnp.float32, jnp.bfloat16


def own_row():
    return (lax.axis_index("x") * 4 + lax.axis_index("zh")) * 2 + lax.axis_index("core")


def slice_kernel(owners, slices, relabels, left, right, out, l_own, r_own, sems):
    row = own_row()
    used = [owners[k] == row for k in range(3)]
    chosen = jnp.int32(0)
    for k in range(3):
        chosen = jnp.where(used[k], slices[k], chosen)
    at_z, at_y = lax.axis_index("za") * 4 + lax.axis_index("zb"), lax.axis_index("y")
    block = jnp.where(used[0], at_z * 4 + at_y, at_y * 8 + at_z)
    block = jnp.where(used[2], (at_z >> 1) * 8 + at_y * 2 + (at_z & 1), block)
    rows = pl.ds(pl.multiple_of(block * 16, 16), 16)
    copies = [
        pltpu.make_async_copy(right.at[0, chosen, 0], r_own.at[0], sems.at[0]),
        pltpu.make_async_copy(right.at[0, chosen, 1], r_own.at[1], sems.at[1]),
        pltpu.make_async_copy(left.at[0, 0, rows], l_own.at[0], sems.at[2]),
        pltpu.make_async_copy(left.at[0, 1, rows], l_own.at[1], sems.at[3]),
    ]
    for copy in copies:
        copy.start()
    q = lax.broadcasted_iota(jnp.int32, (512, 512), 0)
    arrived = (((q >> 3) & 1) << 8) | (((q >> 4) & 15) << 4) | (((q >> 8) & 1) << 3) | (q & 7)
    place = jnp.where(used[1], arrived, q)
    mapping = lax.broadcasted_iota(jnp.int32, (1, 512), 1)
    mapping = jnp.where(used[1], relabels[0:1, :], mapping)
    mapping = jnp.where(used[2], relabels[1:2, :], mapping)
    onehot = jnp.where(place == mapping, 1.0, 0.0).astype(BF16)
    for copy in copies:
        copy.wait()
    both = jnp.concatenate([l_own[0], l_own[1]], axis=0)
    by_real = jnp.dot(both, r_own[0], preferred_element_type=F32)
    by_imag = jnp.dot(both, r_own[1], preferred_element_type=F32)
    real = by_real[:16] - by_imag[16:]
    imag = by_imag[:16] + by_real[16:]
    branch = jnp.concatenate([real, imag], axis=0).astype(BF16)
    moved = lax.dot_general(branch, onehot, (((1,), (1,)), ((), ())), preferred_element_type=F32)
    halves = jnp.concatenate([moved[:8], moved[16:24], moved[8:16], moved[24:]], axis=0)
    moved = jnp.where(used[0], halves, moved).astype(BF16)
    for c in range(4):
        for h in range(2):
            out[c * 2 + h] = moved[h * 16 : h * 16 + 16, c * 128 : c * 128 + 128]


VMEM = pl.BlockSpec(memory_space=pltpu.VMEM)
HBM = pl.BlockSpec(memory_space=pl.ANY)
SMEM = pl.BlockSpec(memory_space=pltpu.SMEM)
SMALL = pltpu.CompilerParams(vmem_limit_bytes=16 << 20)


def branch_slice(owners, slices, relabels, left, right):
    return pl.pallas_call(
        slice_kernel,
        in_specs=[SMEM, SMEM, VMEM, HBM, HBM],
        out_specs=VMEM,
        scratch_shapes=[
            pltpu.VMEM((2, 16, 512), BF16),
            pltpu.VMEM((2, 512, 512), BF16),
            pltpu.SemaphoreType.DMA((4,)),
        ],
        out_shape=jax.ShapeDtypeStruct((8, *TILE), BF16),
        name="branch_slice",
    )(owners, slices, relabels, left, right)


def pick_kernel(by_zh, owners, tiles, out):
    for k in range(3):
        at_x, at_zh, at_core = owners[k] >> 3, (owners[k] >> 1) & 3, owners[k] & 1
        tile = tiles[at_zh, k] if by_zh else tiles[at_x * 2 + at_core]
        for i in range(out.shape[0]):
            out[i, k] = tile


def pick(owners, tiles, by_zh, count):
    return pl.pallas_call(
        functools.partial(pick_kernel, by_zh),
        in_specs=[SMEM, VMEM],
        out_specs=VMEM,
        out_shape=jax.ShapeDtypeStruct((count, 3, *TILE), BF16),
        compiler_params=SMALL,
        name="pick",
    )(owners, tiles)


def pack_kernel(tiles, out):
    half = lax.axis_index("za") * 4
    for j in range(12):
        tile = tiles[half + j, 0] if j < 4 else tiles[j - 4, 1]
        for i in range(16):
            out[i, j] = tile
    for j in range(8):
        tile = tiles[j, 2]
        for x in range(4):
            out[x * 4 + j // 2, 12 + j % 2] = tile


def pack(tiles):
    return pl.pallas_call(
        pack_kernel,
        in_specs=[VMEM],
        out_specs=VMEM,
        out_shape=jax.ShapeDtypeStruct((16, 14, *TILE), BF16),
        compiler_params=SMALL,
        name="pack",
    )(tiles)


def first_kernel(held, *refs):
    *stems, out = refs
    branch = jnp.concatenate([held[c * 4 : c * 4 + 4, :4].reshape(256, 128) for c in range(4)], axis=1)
    results = []
    for stem in stems:
        both = jnp.concatenate([stem[0], stem[1]], axis=1)
        by = jnp.dot(branch, both, preferred_element_type=F32).reshape(16, 2, 8, 256)
        real = by[:, 0, :, :128] - by[:, 1, :, 128:]
        imag = by[:, 0, :, 128:] + by[:, 1, :, :128]
        results.append((real, imag))
    core, ahead = lax.axis_index("core"), lax.axis_index("za") == 1
    for flip in range(2):
        target = jnp.bitwise_xor(core, flip)
        for part in range(2):
            near, far = results[flip][part], results[2 + flip][part]
            low, high = jnp.where(ahead, far, near), jnp.where(ahead, near, far)
            tiles = jnp.concatenate([low, high], axis=1).astype(BF16)
            for y in range(4):
                for zb in range(4):
                    out[target, zb * 4 + y, part] = tiles[y * 4 + zb]


def first_contract(held, stems):
    return pl.pallas_call(
        first_kernel,
        in_specs=[VMEM] * 5,
        out_specs=VMEM,
        out_shape=jax.ShapeDtypeStruct((2, 16, 2, *TILE), BF16),
        compiler_params=SMALL,
        name="first_contract",
    )(held, *stems)


def make_contract_kernel(shifted):
    def kernel(own, other, state, out):
        at_y = lax.axis_index("y")
        parts = []
        for ref in (own, other):
            if shifted:
                columns = [
                    jnp.concatenate(
                        [ref[(at_y - y) & 3, c * 4 : c * 4 + 4].reshape(128, 128) for y in range(4)], axis=0
                    )
                    for c in range(4)
                ]
            else:
                columns = [ref[c * 4 : c * 4 + 4].reshape(512, 128) for c in range(4)]
            parts.append(jnp.concatenate(columns, axis=1))
        both = jnp.concatenate([state[:, 0].reshape(512, 128), state[:, 1].reshape(512, 128)], axis=1)
        by_own = jnp.dot(parts[0], both, preferred_element_type=F32)
        by_other = jnp.dot(parts[1], both, preferred_element_type=F32)
        swapped = lax.axis_index("core") == 1
        by_real = jnp.where(swapped, by_other, by_own)
        by_imag = jnp.where(swapped, by_own, by_other)
        real = (by_real[:, :128] - by_imag[:, 128:]).astype(BF16)
        imag = (by_real[:, 128:] + by_imag[:, :128]).astype(BF16)
        if len(out.shape) == 4:
            out[:, 0] = real.reshape(32, *TILE)
            out[:, 1] = imag.reshape(32, *TILE)
        else:
            out[0] = real
            out[1] = imag

    return kernel


def contract(own, other, state, shape, shifted):
    return pl.pallas_call(
        make_contract_kernel(shifted),
        in_specs=[VMEM] * 3,
        out_specs=VMEM,
        out_shape=jax.ShapeDtypeStruct(shape, BF16),
        compiler_params=SMALL,
        name="contract",
    )(own, other, state)


def send(blocks, axes):
    return lax.all_to_all(blocks, axes, 0, 0, tiled=True)


def steps(stem, left, right, owners, slices, relabels):
    across = lax.ppermute(stem, "za", FLIP)
    beside = lax.ppermute(stem, "core", FLIP)
    both = lax.ppermute(across, "core", FLIP)
    made = branch_slice(owners, slices, relabels, left, right)
    tiles = send(made, SPREAD)
    picked = pick(owners, tiles, False, 4)
    shares = send(picked, "zh")
    picked = pick(owners, shares, True, 8)
    shares = send(picked, LINE)
    packed = pack(shares)
    held = send(packed, PLANE)
    state = first_contract(held, (stem, beside, across, both)).reshape(32, 2, *TILE)
    state = send(state, NEAR)
    own, last = held[:, 4:12], held[:, 12:]
    other = lax.ppermute(own, "core", FLIP)
    state = contract(own, other, state, (32, 2, *TILE), False)
    state = send(state, COL)
    pieces = [last]
    for offset in (1, 2, 3):
        pieces.append(lax.ppermute(last, "y", [(i, (i + offset) % 4) for i in range(4)]))
    last = jnp.stack(pieces)
    other = lax.ppermute(last, "core", FLIP)
    return contract(last, other, state, (2, 512, 128), True)


def solution(mesh):
    fine = Mesh(mesh.devices.reshape([size for _, size in PARTS]), ALL)
    in_specs = (
        P(None, None, ALL),
        P(ROW, None, None, None),
        P(ROW, None, None, None, None),
        P(),
        P(),
        P(),
    )
    return jax.shard_map(steps, mesh=fine, in_specs=in_specs, out_specs=P(None, None, ALL), check_vma=False)
```

```python
import functools

import jax
import jax.numpy as jnp
from jax import lax
from jax.experimental import pallas as pl
from jax.experimental.pallas import tpu as pltpu
from jax.sharding import Mesh
from jax.sharding import PartitionSpec as P

PARTS = (("x", 4), ("zh", 4), ("core", 2), ("za", 2), ("zb", 4), ("y", 4))
ALL = tuple(name for name, _ in PARTS)
ROW, COL = ALL[:3], ALL[3:]
SPREAD, LINE, PLANE, NEAR = ("x", "core"), ("za", "zb"), ("x", "y"), ("core", "zb", "y")
TILE = (16, 128)
FLIP = [(0, 1), (1, 0)]
F32, BF16 = jnp.float32, jnp.bfloat16


def own_row():
    return (lax.axis_index("x") * 4 + lax.axis_index("zh")) * 2 + lax.axis_index("core")


def slice_kernel(owners_in, slices_in, relabels_in, left, right, out, owners, slices, relabels, l_own, r_own, sems):
    at_z, at_y = lax.axis_index("za") * 4 + lax.axis_index("zb"), lax.axis_index("y")
    blocks = (at_z * 4 + at_y, at_y * 8 + at_z, (at_z >> 1) * 8 + at_y * 2 + (at_z & 1))
    pairs = [(owners_in, owners), (slices_in, slices), (relabels_in, relabels)]
    pairs += [(left.at[0, :, pl.ds(pl.multiple_of(block * 16, 16), 16)], l_own.at[k]) for k, block in enumerate(blocks)]
    pairs += [(right.at[0, s], r_own.at[s]) for s in range(2)]
    copies = [pltpu.make_async_copy(source, target, sems.at[i]) for i, (source, target) in enumerate(pairs)]
    for copy in copies:
        copy.start()
    for copy in copies[:3]:
        copy.wait()
    row = own_row()
    used = [owners[k] == row for k in range(3)]
    chosen, place_in_order = jnp.int32(0), jnp.int32(0)
    for k in range(3):
        chosen = jnp.where(used[k], slices[k], chosen)
        place_in_order = jnp.where(used[k], k, place_in_order)
    q = lax.broadcasted_iota(jnp.int32, (512, 512), 0)
    arrived = (((q >> 3) & 1) << 8) | (((q >> 4) & 15) << 4) | (((q >> 8) & 1) << 3) | (q & 7)
    place = jnp.where(used[1], arrived, q)
    mapping = lax.broadcasted_iota(jnp.int32, (1, 512), 1)
    mapping = jnp.where(used[1], relabels[0:1, :], mapping)
    mapping = jnp.where(used[2], relabels[1:2, :], mapping)
    onehot = jnp.where(place == mapping, 1.0, 0.0).astype(BF16)
    for copy in copies[3:]:
        copy.wait()
    both = jnp.concatenate([l_own[place_in_order, 0], l_own[place_in_order, 1]], axis=0)
    by_real = jnp.dot(both, r_own[chosen, 0], preferred_element_type=F32)
    by_imag = jnp.dot(both, r_own[chosen, 1], preferred_element_type=F32)
    real = by_real[:16] - by_imag[16:]
    imag = by_imag[:16] + by_real[16:]
    branch = jnp.concatenate([real, imag], axis=0).astype(BF16)
    moved = lax.dot_general(branch, onehot, (((1,), (1,)), ((), ())), preferred_element_type=F32)
    halves = jnp.concatenate([moved[:8], moved[16:24], moved[8:16], moved[24:]], axis=0)
    moved = jnp.where(used[0], halves, moved).astype(BF16)
    for c in range(4):
        for h in range(2):
            out[c * 2 + h] = moved[h * 16 : h * 16 + 16, c * 128 : c * 128 + 128]


VMEM = pl.BlockSpec(memory_space=pltpu.VMEM)
HBM = pl.BlockSpec(memory_space=pl.ANY)
SMEM = pl.BlockSpec(memory_space=pltpu.SMEM)
SMALL = pltpu.CompilerParams(vmem_limit_bytes=16 << 20)


def branch_slice(owners, slices, relabels, left, right):
    return pl.pallas_call(
        slice_kernel,
        in_specs=[HBM] * 5,
        out_specs=VMEM,
        scratch_shapes=[
            pltpu.SMEM((3,), jnp.int32),
            pltpu.SMEM((3,), jnp.int32),
            pltpu.VMEM((2, 512), jnp.int32),
            pltpu.VMEM((3, 2, 16, 512), BF16),
            pltpu.VMEM((2, 2, 512, 512), BF16),
            pltpu.SemaphoreType.DMA((8,)),
        ],
        out_shape=jax.ShapeDtypeStruct((8, *TILE), BF16),
        name="branch_slice",
    )(owners, slices, relabels, left, right)


def pick_kernel(by_zh, owners, tiles, out):
    for k in range(3):
        at_x, at_zh, at_core = owners[k] >> 3, (owners[k] >> 1) & 3, owners[k] & 1
        tile = tiles[at_zh, k] if by_zh else tiles[at_x * 2 + at_core]
        for i in range(out.shape[0]):
            out[i, k] = tile


def pick(owners, tiles, by_zh, count):
    return pl.pallas_call(
        functools.partial(pick_kernel, by_zh),
        in_specs=[SMEM, VMEM],
        out_specs=VMEM,
        out_shape=jax.ShapeDtypeStruct((count, 3, *TILE), BF16),
        compiler_params=SMALL,
        name="pick",
    )(owners, tiles)


def pack_kernel(tiles, out):
    half = lax.axis_index("za") * 4
    for j in range(12):
        tile = tiles[half + j, 0] if j < 4 else tiles[j - 4, 1]
        for i in range(16):
            out[i, j] = tile
    for j in range(8):
        tile = tiles[j, 2]
        for x in range(4):
            out[x * 4 + j // 2, 12 + j % 2] = tile


def pack(tiles):
    return pl.pallas_call(
        pack_kernel,
        in_specs=[VMEM],
        out_specs=VMEM,
        out_shape=jax.ShapeDtypeStruct((16, 14, *TILE), BF16),
        compiler_params=SMALL,
        name="pack",
    )(tiles)


def first_kernel(held, *refs):
    *stems, out = refs
    branch = jnp.concatenate([held[c * 4 : c * 4 + 4, :4].reshape(256, 128) for c in range(4)], axis=1)
    results = []
    for stem in stems:
        both = jnp.concatenate([stem[0], stem[1]], axis=1)
        by = jnp.dot(branch, both, preferred_element_type=F32).reshape(16, 2, 8, 256)
        real = by[:, 0, :, :128] - by[:, 1, :, 128:]
        imag = by[:, 0, :, 128:] + by[:, 1, :, :128]
        results.append((real, imag))
    core, ahead = lax.axis_index("core"), lax.axis_index("za") == 1
    for flip in range(2):
        target = jnp.bitwise_xor(core, flip)
        for part in range(2):
            near, far = results[flip][part], results[2 + flip][part]
            low, high = jnp.where(ahead, far, near), jnp.where(ahead, near, far)
            tiles = jnp.concatenate([low, high], axis=1).astype(BF16)
            for y in range(4):
                for zb in range(4):
                    out[target, zb * 4 + y, part] = tiles[y * 4 + zb]


def first_contract(held, stems):
    return pl.pallas_call(
        first_kernel,
        in_specs=[VMEM] * 5,
        out_specs=VMEM,
        out_shape=jax.ShapeDtypeStruct((2, 16, 2, *TILE), BF16),
        compiler_params=SMALL,
        name="first_contract",
    )(held, *stems)


def make_contract_kernel(shifted):
    def kernel(own, other, state, out):
        at_y = lax.axis_index("y")
        parts = []
        for ref in (own, other):
            if shifted:
                columns = [
                    jnp.concatenate(
                        [ref[(at_y - y) & 3, c * 4 : c * 4 + 4].reshape(128, 128) for y in range(4)], axis=0
                    )
                    for c in range(4)
                ]
            else:
                columns = [ref[c * 4 : c * 4 + 4].reshape(512, 128) for c in range(4)]
            parts.append(jnp.concatenate(columns, axis=1))
        both = jnp.concatenate([state[:, 0].reshape(512, 128), state[:, 1].reshape(512, 128)], axis=1)
        by_own = jnp.dot(parts[0], both, preferred_element_type=F32)
        by_other = jnp.dot(parts[1], both, preferred_element_type=F32)
        swapped = lax.axis_index("core") == 1
        by_real = jnp.where(swapped, by_other, by_own)
        by_imag = jnp.where(swapped, by_own, by_other)
        real = (by_real[:, :128] - by_imag[:, 128:]).astype(BF16)
        imag = (by_real[:, 128:] + by_imag[:, :128]).astype(BF16)
        if len(out.shape) == 4:
            out[:, 0] = real.reshape(32, *TILE)
            out[:, 1] = imag.reshape(32, *TILE)
        else:
            out[0] = real
            out[1] = imag

    return kernel


def contract(own, other, state, shape, shifted):
    return pl.pallas_call(
        make_contract_kernel(shifted),
        in_specs=[VMEM] * 3,
        out_specs=VMEM,
        out_shape=jax.ShapeDtypeStruct(shape, BF16),
        compiler_params=SMALL,
        name="contract",
    )(own, other, state)


def send(blocks, axes):
    return lax.all_to_all(blocks, axes, 0, 0, tiled=True)


def steps(stem, left, right, owners, slices, relabels):
    across = lax.ppermute(stem, "za", FLIP)
    beside = lax.ppermute(stem, "core", FLIP)
    both = lax.ppermute(across, "core", FLIP)
    made = branch_slice(owners, slices, relabels, left, right)
    tiles = send(made, SPREAD)
    picked = pick(owners, tiles, False, 4)
    shares = send(picked, "zh")
    picked = pick(owners, shares, True, 8)
    shares = send(picked, LINE)
    packed = pack(shares)
    held = send(packed, PLANE)
    state = first_contract(held, (stem, beside, across, both)).reshape(32, 2, *TILE)
    state = send(state, NEAR)
    own, last = held[:, 4:12], held[:, 12:]
    other = lax.ppermute(own, "core", FLIP)
    state = contract(own, other, state, (32, 2, *TILE), False)
    state = send(state, COL)
    pieces = [last]
    for offset in (1, 2, 3):
        pieces.append(lax.ppermute(last, "y", [(i, (i + offset) % 4) for i in range(4)]))
    last = jnp.stack(pieces)
    other = lax.ppermute(last, "core", FLIP)
    return contract(last, other, state, (2, 512, 128), True)


def solution(mesh):
    fine = Mesh(mesh.devices.reshape([size for _, size in PARTS]), ALL)
    in_specs = (
        P(None, None, ALL),
        P(ROW, None, None, None),
        P(ROW, None, None, None, None),
        P(),
        P(),
        P(),
    )
    return jax.shard_map(steps, mesh=fine, in_specs=in_specs, out_specs=P(None, None, ALL), check_vma=False)
```

```python
import functools

import jax
import jax.numpy as jnp
from jax import lax
from jax.experimental import pallas as pl
from jax.experimental.pallas import tpu as pltpu
from jax.sharding import Mesh
from jax.sharding import PartitionSpec as P

PARTS = (("x", 4), ("zh", 4), ("core", 2), ("za", 2), ("zb", 4), ("y", 4))
ALL = tuple(name for name, _ in PARTS)
ROW, COL = ALL[:3], ALL[3:]
SPREAD, LINE, PLANE, NEAR = ("x", "core"), ("za", "zb"), ("x", "y"), ("core", "zb", "y")
TILE = (16, 128)
FLIP = [(0, 1), (1, 0)]
F32, BF16 = jnp.float32, jnp.bfloat16


def own_row():
    return (lax.axis_index("x") * 4 + lax.axis_index("zh")) * 2 + lax.axis_index("core")


def slice_kernel(owners_in, slices_in, relabels_in, left, right, out, owners, slices, relabels, l_own, r_own, sems):
    at_z, at_y = lax.axis_index("za") * 4 + lax.axis_index("zb"), lax.axis_index("y")
    blocks = (at_z * 4 + at_y, at_y * 8 + at_z, (at_z >> 1) * 8 + at_y * 2 + (at_z & 1))
    pairs = [(owners_in, owners), (slices_in, slices), (relabels_in, relabels)]
    pairs += [(left.at[0, :, pl.ds(pl.multiple_of(block * 16, 16), 16)], l_own.at[k]) for k, block in enumerate(blocks)]
    depths = [pl.ds(i * 128, 128) for i in range(4)]
    pairs += [(right.at[0, s, :, depth], r_own.at[s, :, depth]) for depth in depths for s in range(2)]
    copies = [pltpu.make_async_copy(source, target, sems.at[i]) for i, (source, target) in enumerate(pairs)]
    for copy in copies:
        copy.start()
    for copy in copies[:3]:
        copy.wait()
    row = own_row()
    used = [owners[k] == row for k in range(3)]
    chosen, place_in_order = jnp.int32(0), jnp.int32(0)
    for k in range(3):
        chosen = jnp.where(used[k], slices[k], chosen)
        place_in_order = jnp.where(used[k], k, place_in_order)
    q = lax.broadcasted_iota(jnp.int32, (512, 512), 0)
    arrived = (((q >> 3) & 1) << 8) | (((q >> 4) & 15) << 4) | (((q >> 8) & 1) << 3) | (q & 7)
    place = jnp.where(used[1], arrived, q)
    mapping = lax.broadcasted_iota(jnp.int32, (1, 512), 1)
    mapping = jnp.where(used[1], relabels[0:1, :], mapping)
    mapping = jnp.where(used[2], relabels[1:2, :], mapping)
    onehot = jnp.where(place == mapping, 1.0, 0.0).astype(BF16)
    for copy in copies[3:6]:
        copy.wait()
    both = jnp.concatenate([l_own[place_in_order, 0], l_own[place_in_order, 1]], axis=0)
    by_real, by_imag = jnp.zeros((32, 512), F32), jnp.zeros((32, 512), F32)
    for i, depth in enumerate(depths):
        for copy in copies[6 + 2 * i : 8 + 2 * i]:
            copy.wait()
        some = both[:, i * 128 : i * 128 + 128]
        by_real += jnp.dot(some, r_own[chosen, 0, depth], preferred_element_type=F32)
        by_imag += jnp.dot(some, r_own[chosen, 1, depth], preferred_element_type=F32)
    real = by_real[:16] - by_imag[16:]
    imag = by_imag[:16] + by_real[16:]
    branch = jnp.concatenate([real, imag], axis=0).astype(BF16)
    moved = lax.dot_general(branch, onehot, (((1,), (1,)), ((), ())), preferred_element_type=F32)
    halves = jnp.concatenate([moved[:8], moved[16:24], moved[8:16], moved[24:]], axis=0)
    moved = jnp.where(used[0], halves, moved).astype(BF16)
    for c in range(4):
        for h in range(2):
            out[c * 2 + h] = moved[h * 16 : h * 16 + 16, c * 128 : c * 128 + 128]


VMEM = pl.BlockSpec(memory_space=pltpu.VMEM)
HBM = pl.BlockSpec(memory_space=pl.ANY)
SMEM = pl.BlockSpec(memory_space=pltpu.SMEM)
SMALL = pltpu.CompilerParams(vmem_limit_bytes=16 << 20)


def branch_slice(owners, slices, relabels, left, right):
    return pl.pallas_call(
        slice_kernel,
        in_specs=[HBM] * 5,
        out_specs=VMEM,
        scratch_shapes=[
            pltpu.SMEM((3,), jnp.int32),
            pltpu.SMEM((3,), jnp.int32),
            pltpu.VMEM((2, 512), jnp.int32),
            pltpu.VMEM((3, 2, 16, 512), BF16),
            pltpu.VMEM((2, 2, 512, 512), BF16),
            pltpu.SemaphoreType.DMA((14,)),
        ],
        out_shape=jax.ShapeDtypeStruct((8, *TILE), BF16),
        name="branch_slice",
    )(owners, slices, relabels, left, right)


def pick_kernel(by_zh, owners, tiles, out):
    for k in range(3):
        at_x, at_zh, at_core = owners[k] >> 3, (owners[k] >> 1) & 3, owners[k] & 1
        tile = tiles[at_zh, k] if by_zh else tiles[at_x * 2 + at_core]
        for i in range(out.shape[0]):
            out[i, k] = tile


def pick(owners, tiles, by_zh, count):
    return pl.pallas_call(
        functools.partial(pick_kernel, by_zh),
        in_specs=[SMEM, VMEM],
        out_specs=VMEM,
        out_shape=jax.ShapeDtypeStruct((count, 3, *TILE), BF16),
        compiler_params=SMALL,
        name="pick",
    )(owners, tiles)


def pack_kernel(tiles, out, block, sems):
    half = lax.axis_index("za") * 4
    for j in range(12):
        tile = tiles[half + j, 0] if j < 4 else tiles[j - 4, 1]
        for y in range(4):
            block[y, j] = tile
    for j in range(8):
        block[j // 2, 12 + j % 2] = tiles[j, 2]
    copies = [pltpu.make_async_copy(block, out.at[pl.ds(x * 4, 4)], sems.at[x]) for x in range(4)]
    for copy in copies:
        copy.start()
    for copy in copies:
        copy.wait()


def pack(tiles):
    return pl.pallas_call(
        pack_kernel,
        in_specs=[VMEM],
        out_specs=HBM,
        scratch_shapes=[pltpu.VMEM((4, 14, *TILE), BF16), pltpu.SemaphoreType.DMA((4,))],
        out_shape=jax.ShapeDtypeStruct((16, 14, *TILE), BF16),
        compiler_params=SMALL,
        name="pack",
    )(tiles)


def first_kernel(held, *refs):
    *stems, out = refs
    branch = jnp.concatenate([held[c * 4 : c * 4 + 4, :4].reshape(256, 128) for c in range(4)], axis=1)
    results = []
    for stem in stems:
        both = jnp.concatenate([stem[0], stem[1]], axis=1)
        by = jnp.dot(branch, both, preferred_element_type=F32).reshape(16, 2, 8, 256)
        real = by[:, 0, :, :128] - by[:, 1, :, 128:]
        imag = by[:, 0, :, 128:] + by[:, 1, :, :128]
        results.append((real, imag))
    core, ahead = lax.axis_index("core"), lax.axis_index("za") == 1
    for flip in range(2):
        target = jnp.bitwise_xor(core, flip)
        for part in range(2):
            near, far = results[flip][part], results[2 + flip][part]
            low, high = jnp.where(ahead, far, near), jnp.where(ahead, near, far)
            tiles = jnp.concatenate([low, high], axis=1).astype(BF16)
            for y in range(4):
                for zb in range(4):
                    out[target, zb * 4 + y, part] = tiles[y * 4 + zb]


def first_contract(held, stems):
    return pl.pallas_call(
        first_kernel,
        in_specs=[VMEM] * 5,
        out_specs=VMEM,
        out_shape=jax.ShapeDtypeStruct((2, 16, 2, *TILE), BF16),
        compiler_params=SMALL,
        name="first_contract",
    )(held, *stems)


def make_contract_kernel(shifted):
    def kernel(own, other, state, out):
        at_y = lax.axis_index("y")
        parts = []
        for ref in (own, other):
            if shifted:
                columns = [
                    jnp.concatenate(
                        [ref[(at_y - y) & 3, c * 4 : c * 4 + 4].reshape(128, 128) for y in range(4)], axis=0
                    )
                    for c in range(4)
                ]
            else:
                columns = [ref[c * 4 : c * 4 + 4].reshape(512, 128) for c in range(4)]
            parts.append(jnp.concatenate(columns, axis=1))
        both = jnp.concatenate([state[:, 0].reshape(512, 128), state[:, 1].reshape(512, 128)], axis=1)
        by_own = jnp.dot(parts[0], both, preferred_element_type=F32)
        by_other = jnp.dot(parts[1], both, preferred_element_type=F32)
        swapped = lax.axis_index("core") == 1
        by_real = jnp.where(swapped, by_other, by_own)
        by_imag = jnp.where(swapped, by_own, by_other)
        real = (by_real[:, :128] - by_imag[:, 128:]).astype(BF16)
        imag = (by_real[:, 128:] + by_imag[:, :128]).astype(BF16)
        if len(out.shape) == 4:
            out[:, 0] = real.reshape(32, *TILE)
            out[:, 1] = imag.reshape(32, *TILE)
        else:
            out[0] = real
            out[1] = imag

    return kernel


def contract(own, other, state, shape, shifted):
    return pl.pallas_call(
        make_contract_kernel(shifted),
        in_specs=[VMEM] * 3,
        out_specs=VMEM,
        out_shape=jax.ShapeDtypeStruct(shape, BF16),
        compiler_params=SMALL,
        name="contract",
    )(own, other, state)


def send(blocks, axes):
    return lax.all_to_all(blocks, axes, 0, 0, tiled=True)


def steps(stem, left, right, owners, slices, relabels):
    across = lax.ppermute(stem, "za", FLIP)
    beside = lax.ppermute(stem, "core", FLIP)
    both = lax.ppermute(across, "core", FLIP)
    made = branch_slice(owners, slices, relabels, left, right)
    tiles = send(made, SPREAD)
    picked = pick(owners, tiles, False, 4)
    shares = send(picked, "zh")
    picked = pick(owners, shares, True, 8)
    shares = send(picked, LINE)
    packed = pack(shares)
    held = send(packed, PLANE)
    state = first_contract(held, (stem, beside, across, both)).reshape(32, 2, *TILE)
    state = send(state, NEAR)
    own, last = held[:, 4:12], held[:, 12:]
    other = lax.ppermute(own, "core", FLIP)
    state = contract(own, other, state, (32, 2, *TILE), False)
    state = send(state, COL)
    pieces = [last]
    for offset in (1, 2, 3):
        pieces.append(lax.ppermute(last, "y", [(i, (i + offset) % 4) for i in range(4)]))
    last = jnp.stack(pieces)
    other = lax.ppermute(last, "core", FLIP)
    return contract(last, other, state, (2, 512, 128), True)


def solution(mesh):
    fine = Mesh(mesh.devices.reshape([size for _, size in PARTS]), ALL)
    in_specs = (
        P(None, None, ALL),
        P(ROW, None, None, None),
        P(ROW, None, None, None, None),
        P(),
        P(),
        P(),
    )
    return jax.shard_map(steps, mesh=fine, in_specs=in_specs, out_specs=P(None, None, ALL), check_vma=False)
```
